128 devices in a mesh: tomo: 16 (over y, z), cls: 8 (over x, core).
Axes of the slice: x: 4, y: 4, z: 4, core: 2. Of those that a mesh axis runs over, the one named last changes fastest.
Arguments:
- particles: bfloat16 [1024, 64, 4096], P(('tomo', 'cls')), may hold values from -6 to 6
- inverse_noise: float32 [1024], P(('tomo', 'cls')), may hold values from 0.005 to 0.04
- tomogram: int32 [1024], P(('tomo', 'cls')), may hold values from 0 to 63, as said below
- candidates: int32 [1024, 4], P(('tomo', 'cls')), may hold values from 0 to 31, as said below
- rotations: int32 [1024, 8], P(('tomo', 'cls')), may hold values from 0 to 15, as said below
- wedge: int32 [64, 32, 32], P('tomo'), may hold values from 0 to 1
- references: bfloat16 [32, 16, 65536], P('cls'), may hold values from -8 to 8
Outputs:
- posterior: float32 [1024, 32], P(('tomo', 'cls'))
- class_sums: float32 [32, 16, 65536], P('cls', None, 'tomo')
- wedge_sums: float32 [32, 16, 1024], P('cls', None, 'tomo')
The draws below stay inside these ranges and needn't reach their ends.
Inputs may be any that keep to these rules, and one draw needn't show every extreme that they name: The tomogram of a particle held by index t of tomo is one of t * 4 to t * 4 + 3. `candidates`: each particle lists 4 different classes: two held by each of two different indices of cls (class c is held by index c // 4). Of the 8 particles of one device, at most 4 list classes of any one index of cls, and in every row of tomo one index of cls is listed by exactly 4 particles of every device of that row. `rotations`: 8 different indices for each particle.
All inputs are finite; a program needn't handle non-finite values.
Results may differ from the reference program's by a relative error of at most 0.009.
Values may be sent and summed in bfloat16 or wider, within the bound.
No kernel may reach another device: no remote copies, remote signals or barrier semaphores. Data moves between devices by JAX's collectives and lax.ppermute only.
A program may use at most 256 MiB of HBM per device.

```python
import math
import jax
import jax.numpy as jnp
from jax import lax

VOX = 64
KB = 32
CLASSES = 32
NSET = 16
ROT = 8
CAND = 4
PART_DEV = 8
TOMO_DEV = 4
CLS_DEV = 4
PARTICLES = 1024
TOMOGRAMS = 64


def volume_of(key, particle_index):
    gaussian = jax.random.normal(jax.random.fold_in(jax.random.fold_in(key, 303), particle_index), (VOX, VOX * VOX), jnp.float32)
    return jnp.clip(gaussian, -6.0, 6.0).astype(jnp.bfloat16)


def candidate_table(key):
    owners = CLASSES // CLS_DEV
    spread = owners - 1
    blocks = PARTICLES // PART_DEV
    row_count = blocks // owners
    capacity = PART_DEV // 2
    sub_keys = jax.random.split(jax.random.fold_in(key, 101), 6)
    hottest = jax.random.randint(sub_keys[0], (row_count,), 0, owners, dtype=jnp.int32)
    hot_block = jnp.repeat(hottest, owners)
    shuffle = jax.vmap(lambda sub_key: jax.random.permutation(sub_key, spread))(jax.random.split(sub_keys[1], blocks)).astype(jnp.int32)
    others = (hot_block[:, None] + 1 + shuffle) % owners
    position = jnp.arange(PART_DEV, dtype=jnp.int32)
    hit_first = jnp.where(position < capacity, position, capacity + 2 * (position - capacity))
    pick_first = jnp.take_along_axis(others, jnp.broadcast_to(hit_first % spread, (blocks, PART_DEV)), axis=1)
    first_owner = jnp.where(position[None, :] < capacity, hot_block[:, None], pick_first)
    hit_second = jnp.where(position < capacity, position, hit_first + 1) % spread
    second_owner = jnp.take_along_axis(others, jnp.broadcast_to(hit_second, (blocks, PART_DEV)), axis=1)
    reorder = jax.vmap(lambda sub_key: jax.random.permutation(sub_key, PART_DEV))(jax.random.split(sub_keys[2], blocks)).astype(jnp.int32)
    first_owner = jnp.take_along_axis(first_owner, reorder, axis=1)
    second_owner = jnp.take_along_axis(second_owner, reorder, axis=1)
    first_pick = jax.random.randint(sub_keys[3], (blocks, PART_DEV, 2), 0, CLS_DEV, dtype=jnp.int32)
    second_pick = (first_pick + 1 + jax.random.randint(sub_keys[4], (blocks, PART_DEV, 2), 0, CLS_DEV - 1, dtype=jnp.int32)) % CLS_DEV
    listed = jnp.stack([first_owner * CLS_DEV + first_pick[..., 0], first_owner * CLS_DEV + second_pick[..., 0], second_owner * CLS_DEV + first_pick[..., 1], second_owner * CLS_DEV + second_pick[..., 1]], axis=-1).reshape(PARTICLES, CAND)
    mixing = jax.vmap(lambda sub_key: jax.random.permutation(sub_key, CAND))(jax.random.split(sub_keys[5], PARTICLES)).astype(jnp.int32)
    return jnp.take_along_axis(listed, mixing, axis=1).astype(jnp.int32)


def rotation_table(key):
    sub_keys = jax.random.split(jax.random.fold_in(key, 202), PARTICLES)
    return jax.vmap(lambda sub_key: jax.random.permutation(sub_key, NSET)[:ROT])(sub_keys).astype(jnp.int32)


def draw_particles(key, part):
    return lax.map(lambda particle_index: volume_of(key, particle_index), jnp.arange(PARTICLES, dtype=jnp.int32))


def draw_tomogram(key, part):
    row_total = TOMOGRAMS // TOMO_DEV
    per_row = PARTICLES // row_total
    row_of = jnp.arange(PARTICLES, dtype=jnp.int32) // per_row
    offset = jax.random.randint(jax.random.fold_in(key, 601), (PARTICLES,), 0, TOMO_DEV, dtype=jnp.int32)
    return (row_of * TOMO_DEV + offset).astype(jnp.int32)


def draw_candidates(key, part):
    return candidate_table(key)


def draw_rotations(key, part):
    return rotation_table(key)


def draw_wedge(key, part):
    upper_slopes = jax.random.randint(jax.random.fold_in(key, 701), (TOMOGRAMS,), 4, 4 * KB + 1, dtype=jnp.int32)
    lower_slopes = jax.random.randint(jax.random.fold_in(key, 702), (TOMOGRAMS,), 4, 4 * KB + 1, dtype=jnp.int32)
    signed = jnp.arange(KB, dtype=jnp.int32) - KB // 2
    magnitude = jnp.abs(signed)
    slope_rows = jnp.where(signed[None, :] >= 0, upper_slopes[:, None], lower_slopes[:, None])
    kept = 8 * magnitude[None, None, :] <= slope_rows[:, :, None] * magnitude[None, :, None]
    return kept.astype(jnp.int32)


def draw_references(key, part):
    gaussian = jax.random.normal(jax.random.fold_in(key, 404), (CLASSES, NSET, 2 * KB ** 3), jnp.float32)
    values = jnp.clip(gaussian, -8.0, 8.0) * 0.7071
    return values.astype(jnp.bfloat16)


def steps_of(stream_key, dims, cuts, low, largest):
    def one(axis_at, parts):
        heights = jax.random.uniform(jax.random.fold_in(jax.random.fold_in(stream_key, 6), axis_at), (parts,), jnp.float32, low / len(cuts), largest / len(cuts))
        return jnp.repeat(jnp.exp(heights), dims[axis_at] // parts).reshape((-1,) + (1,) * (len(dims) - axis_at - 1))

    loudness = one(*cuts[0])
    for cut in cuts[1:]:
        loudness = loudness * one(*cut)
    return loudness


def setup_inputs(seed: int = 0) -> dict:
    arg_keys = jax.random.split(jax.random.key(seed), 8)
    particles = draw_particles(jax.random.fold_in(arg_keys[7], 71), 0)
    inverse_noise = jnp.clip(jnp.exp(math.log(0.04) - 2.0794415 * jax.random.uniform(arg_keys[1], (PARTICLES,), jnp.float32) ** steps_of(arg_keys[1], (PARTICLES,), ((0, 128),), -0.2, 0.2)), 0.005, 0.04)
    tomogram = draw_tomogram(jax.random.fold_in(arg_keys[7], 71), 0)
    candidates = draw_candidates(jax.random.fold_in(arg_keys[7], 71), 0)
    rotations = draw_rotations(jax.random.fold_in(arg_keys[7], 71), 0)
    wedge = draw_wedge(jax.random.fold_in(arg_keys[7], 71), 0)
    references = draw_references(jax.random.fold_in(arg_keys[7], 71), 0)
    return dict(particles=particles, inverse_noise=inverse_noise, tomogram=tomogram, candidates=candidates, rotations=rotations, wedge=wedge, references=references)


HIGHEST = lax.Precision.HIGHEST


def band_spectrum(volume):
    cube = volume.astype(jnp.float32).reshape(VOX, VOX, VOX)
    full = jnp.fft.fftn(cube) / (VOX ** 1.5)
    picks = (jnp.arange(KB) - KB // 2) % VOX
    band_part = full[picks][:, picks][:, :, picks]
    return jnp.stack([jnp.real(band_part), jnp.imag(band_part)])


def reference(particles, inverse_noise, tomogram, candidates, rotations, wedge, references):
    wedge_rows = wedge.reshape(TOMOGRAMS, KB * KB).astype(jnp.float32)
    particle_masks = wedge_rows[tomogram]
    spectra = lax.map(band_spectrum, particles).astype(jnp.bfloat16)
    masked = spectra * particle_masks.reshape(PARTICLES, 1, KB, 1, KB).astype(jnp.bfloat16)
    masked = masked.reshape(PARTICLES, 2 * KB ** 3)
    flat_refs = references.reshape(CLASSES * NSET, 2 * KB ** 3)
    ref_values = references.astype(jnp.float32).reshape(CLASSES * NSET, 2, KB, KB, KB)
    power = jnp.sum(ref_values * ref_values, axis=(1, 3)).reshape(CLASSES * NSET, KB * KB)
    quadratic = jnp.dot(power, wedge_rows.T, precision=HIGHEST)
    pair_codes = candidates[:, :, None] * NSET + rotations[:, None, :]
    penalty = quadratic[pair_codes, tomogram[:, None, None]]
    blocks = PARTICLES // PART_DEV
    block_spec = masked.reshape(blocks, PART_DEV, 2 * KB ** 3)
    block_codes = pair_codes.reshape(blocks, PART_DEV, CAND * ROT)

    def inner_block(pieces):
        spec_piece, code_piece = pieces
        chosen = flat_refs[code_piece.reshape(-1)].reshape(PART_DEV, CAND * ROT, 2 * KB ** 3)
        return jnp.einsum("bq,bhq->bh", spec_piece.astype(jnp.float32), chosen.astype(jnp.float32), precision=HIGHEST)

    inner = lax.map(inner_block, (block_spec, block_codes)).reshape(PARTICLES, CAND, ROT)
    raw = inner - 0.5 * penalty
    logits = inverse_noise[:, None] * raw.reshape(PARTICLES, CAND * ROT)
    posterior = jax.nn.softmax(logits, axis=-1)
    rounded = lax.optimization_barrier(posterior.astype(jnp.bfloat16)).astype(jnp.float32)
    block_weights = rounded.reshape(blocks, PART_DEV, CAND * ROT)
    block_masks = particle_masks.reshape(blocks, PART_DEV, KB * KB)

    def add_block(totals, pieces):
        class_total, wedge_total = totals
        spec_piece, code_piece, weight_piece, mask_piece = pieces
        flat_codes = code_piece.reshape(-1)
        class_terms = weight_piece[:, :, None] * spec_piece.astype(jnp.float32)[:, None, :]
        wedge_terms = weight_piece[:, :, None] * mask_piece[:, None, :]
        class_total = class_total.at[flat_codes].add(class_terms.reshape(PART_DEV * CAND * ROT, 2 * KB ** 3))
        wedge_total = wedge_total.at[flat_codes].add(wedge_terms.reshape(PART_DEV * CAND * ROT, KB * KB))
        return (class_total, wedge_total), None

    start_totals = (jnp.zeros((CLASSES * NSET, 2 * KB ** 3), jnp.float32), jnp.zeros((CLASSES * NSET, KB * KB), jnp.float32))
    (class_total, wedge_total), _ = lax.scan(add_block, start_totals, (block_spec, block_codes, block_weights, block_masks))
    return posterior, class_total.reshape(CLASSES, NSET, 2 * KB ** 3), wedge_total.reshape(CLASSES, NSET, KB * KB)
```

```python
import math

import jax
import jax.numpy as jnp
import numpy as np
from jax import lax
from jax.experimental import pallas as pl
from jax.experimental.pallas import tpu as pltpu
from jax.sharding import PartitionSpec as P


VOX = 64
KB = 32
NSET = 16
ROT = 8
CAND = 4
PART = 8
ROWS = 16
COLS = 8
CLS_DEV = 4
SLICE = 2 * KB**3 // ROWS
EXTRA = 256
WIDTH = SLICE + EXTRA
HALF = WIDTH // 2
CODE_AT = 192


def split_table(table):
    high = table.astype(jnp.bfloat16)
    low = (table - np.asarray(high, np.float32)).astype(jnp.bfloat16)
    return high, low


def dft_constants():
    frequency = np.arange(KB) - KB // 2
    residue = (frequency[:, None] * np.arange(VOX)[None, :]) % VOX
    radians = residue * (2.0 * math.pi / VOX)
    both = (np.stack([np.cos(radians), -np.sin(radians)]) / math.sqrt(VOX)).astype(np.float32)
    depth_table = np.kron(np.eye(4, dtype=np.float32), both.reshape(2 * KB, VOX))
    wz = np.concatenate(split_table(depth_table), axis=0)
    wide = np.einsum("akx,pq->pxakq", both, np.eye(PART, dtype=np.float32))
    wxh, wxl = split_table(wide.reshape(PART * VOX, 2 * KB * PART))
    high, low = split_table(both.reshape(2 * KB, VOX))
    wy = np.concatenate([high, high, low], axis=1)
    return wz, wxh, wxl, wy


def dft_kernel(p_ref, wz_ref, wxh_ref, wxl_ref, wy_ref, mask_ref, ext_ref, out_ref, mid, last):
    step = pl.program_id(0)
    data = p_ref[...].reshape(PART * VOX, 4 * VOX)
    first = lax.dot_general(
        wz_ref[...], data, (((1,), (1,)), ((), ())), preferred_element_type=jnp.float32
    )
    first = first[: 8 * KB] + first[8 * KB :]
    high = first.astype(jnp.bfloat16)
    low = (first - high.astype(jnp.float32)).astype(jnp.bfloat16)
    second = (
        jnp.dot(high, wxh_ref[...], preferred_element_type=jnp.float32)
        + jnp.dot(low, wxh_ref[...], preferred_element_type=jnp.float32)
        + jnp.dot(high, wxl_ref[...], preferred_element_type=jnp.float32)
    )
    for yy in range(4):
        cos_rows = second[yy * 64 : yy * 64 + 32]
        sin_rows = second[yy * 64 + 32 : yy * 64 + 64]
        real = cos_rows[:, :256] - sin_rows[:, 256:]
        imag = sin_rows[:, :256] + cos_rows[:, 256:]
        rows = pl.ds(pl.multiple_of((step * 4 + yy) * KB, KB), KB)
        mid[0, rows, :] = real[:, :128]
        mid[1, rows, :] = real[:, 128:]
        mid[2, rows, :] = imag[:, :128]
        mid[3, rows, :] = imag[:, 128:]

    @pl.when(step == pl.num_programs(0) - 1)
    def _():
        for kz in range(KB):
            values = jnp.concatenate(
                [mid[block, pl.ds(kz, VOX, stride=KB), :] for block in range(4)], axis=1
            )
            top = values.astype(jnp.bfloat16)
            rest = (values - top.astype(jnp.float32)).astype(jnp.bfloat16)
            third = jnp.dot(
                wy_ref[...],
                jnp.concatenate([top, rest, top], axis=0),
                preferred_element_type=jnp.float32,
            )
            real = third[:KB, :256] - third[KB:, 256:]
            imag = third[KB:, :256] + third[:KB, 256:]
            rows = pl.ds(kz, KB, stride=KB)
            last[0, rows, :] = real[:, :128]
            last[1, rows, :] = real[:, 128:]
            last[2, rows, :] = imag[:, :128]
            last[3, rows, :] = imag[:, 128:]
        for block in range(4):
            turned = last[block].T
            for k in range(16):
                kx = (block % 2) * 16 + k
                target = (block // 2) * 8 + kx // 4
                keep = jnp.concatenate([mask_ref[kx]] * 8, axis=1)
                piece = turned[k * PART : (k + 1) * PART, :] * keep
                out_ref[target, :, (kx % 4) * 1024 : (kx % 4 + 1) * 1024] = piece.astype(
                    jnp.bfloat16
                )
        out_ref[:, :, SLICE:] = ext_ref[...]


def spectra_call(particles, mask_tiles, extras):
    wz, wxh, wxl, wy = dft_constants()
    whole = lambda shape: pl.BlockSpec(shape, lambda i: (0,) * len(shape))
    return pl.pallas_call(
        dft_kernel,
        grid=(16,),
        in_specs=[
            pl.BlockSpec((PART, VOX, 256), lambda i: (0, 0, i)),
            whole(wz.shape),
            whole(wxh.shape),
            whole(wxl.shape),
            whole(wy.shape),
            whole((KB, PART, 128)),
            whole((ROWS, PART, EXTRA)),
        ],
        out_specs=whole((ROWS, PART, WIDTH)),
        out_shape=jax.ShapeDtypeStruct((ROWS, PART, WIDTH), jnp.bfloat16),
        scratch_shapes=[
            pltpu.VMEM((4, VOX * KB, 128), jnp.float32),
            pltpu.VMEM((4, KB * KB, 128), jnp.float32),
        ],
        compiler_params=pltpu.CompilerParams(dimension_semantics=("arbitrary",)),
        cost_estimate=pl.CostEstimate(
            flops=20_000_000_000, bytes_accessed=8_000_000, transcendentals=0
        ),
        name="dft",
    )(particles, *(jnp.asarray(t) for t in (wz, wxh, wxl, wy)), mask_tiles, extras)


def score_kernel(base_ref, slots_ref, noise_ref, *refs):
    pieces, out_ref, codes_ref = refs[:-2], refs[-2], refs[-1]
    slots = slots_ref[:, :SLICE]
    codes = slots_ref[:, SLICE + 128 :].astype(jnp.float32).T[CODE_AT - 128 : CODE_AT - 128 + 16]
    codes_ref[...] = codes
    row = lax.broadcasted_iota(jnp.int32, (128, 512), 0)
    col = lax.broadcasted_iota(jnp.int32, (128, 512), 1)
    spread = ((row // KB == col // 128) & (row % KB == col % KB)).astype(jnp.bfloat16)
    keep = jnp.dot(
        slots_ref[:, SLICE : SLICE + 128], spread, preferred_element_type=jnp.float32
    ).astype(jnp.bfloat16)
    chosen = [jnp.zeros((NSET, 128), jnp.float32) for _ in range(CAND)]
    contract = (((1,), (1,)), ((), ()))
    for index, (slot, offset) in enumerate(PIECES):
        ref = pieces[index]
        count = ref.shape[0]
        inner = lax.dot_general(ref[...], slots, contract, preferred_element_type=jnp.float32)
        sums = []
        for k in range(4):
            total = jnp.zeros((count, 128), jnp.float32)
            for j in range(8):
                at = k * 1024 + j * 128
                value = ref[:, at : at + 128].astype(jnp.float32)
                total = total + value * value
            sums.append(total)
        power = jnp.concatenate(sums, axis=1)
        one = power.astype(jnp.bfloat16)
        left = power - one.astype(jnp.float32)
        two = left.astype(jnp.bfloat16)
        three = (left - two.astype(jnp.float32)).astype(jnp.bfloat16)
        stacked = jnp.concatenate([one, two, three], axis=0)
        penalty = lax.dot_general(stacked, keep, contract, preferred_element_type=jnp.float32)
        penalty = (penalty[2 * count :] + penalty[count : 2 * count]) + penalty[:count]
        table = inner - 0.5 * penalty
        for local in range(count // NSET):
            label = (base_ref[slot] * CLS_DEV + offset + local).astype(jnp.float32)
            block = table[local * NSET : (local + 1) * NSET]
            for j in range(CAND):
                chosen[j] = chosen[j] + jnp.where(codes[j : j + 1] == label, block, 0.0)
    copies = lax.broadcasted_iota(jnp.int32, (NSET, 128), 0).astype(jnp.float32)
    for r in range(ROT):
        hit = codes[CAND + r : CAND + r + 1] == copies
        for j in range(CAND):
            out_ref[j * ROT + r : j * ROT + r + 1, :] = jnp.sum(
                jnp.where(hit, chosen[j], 0.0), axis=0, keepdims=True
            )
    out_ref[CAND * ROT :, :] = noise_ref[...]


PIECES = ((0, 0), (1, 0), (2, 0), (3, 0), (3, 2), (4, 0), (5, 0), (6, 0), (7, 0), (7, 2))


def score_call(bases, slots, noise_rows, pieces):
    vmem = pl.BlockSpec(memory_space=pltpu.VMEM)
    return pl.pallas_call(
        score_kernel,
        in_specs=[pl.BlockSpec(memory_space=pltpu.SMEM)] + [vmem] * (2 + len(pieces)),
        out_specs=(vmem, vmem),
        out_shape=(
            jax.ShapeDtypeStruct((CAND * ROT + 8, 128), jnp.float32),
            jax.ShapeDtypeStruct((16, 128), jnp.float32),
        ),
        cost_estimate=pl.CostEstimate(
            flops=1_000_000_000, bytes_accessed=6_000_000, transcendentals=0
        ),
        name="score",
    )(bases, slots, noise_rows, *pieces)


def softmax_kernel(at_ref, parts_ref, codes_ref, post_ref, coef_ref, turned):
    total = parts_ref[0]
    for row in range(1, ROWS):
        total = total + parts_ref[row]
    logits = total[CAND * ROT : CAND * ROT + 1] * total[: CAND * ROT]
    peak = jnp.max(logits, axis=0, keepdims=True)
    weight = jnp.exp(logits - peak)
    posterior = weight / jnp.sum(weight, axis=0, keepdims=True)
    padded = jnp.concatenate([posterior, jnp.zeros((96, 128), jnp.float32)], axis=0)
    turned[...] = padded.T
    own = turned[pl.ds(pl.multiple_of(at_ref[0] * PART, PART), PART), :]
    post_ref[...] = own[:, : CAND * ROT]
    rounded = posterior.astype(jnp.bfloat16).astype(jnp.float32)
    codes = codes_ref[...]
    copies = lax.broadcasted_iota(jnp.int32, (NSET, 128), 0).astype(jnp.float32)
    spread = []
    for j in range(CAND):
        value = jnp.zeros((NSET, 128), jnp.float32)
        for r in range(ROT):
            hit = codes[CAND + r : CAND + r + 1] == copies
            value = value + jnp.where(hit, rounded[j * ROT + r : j * ROT + r + 1], 0.0)
        spread.append(value)
    for label in range(COLS * CLS_DEV):
        value = jnp.zeros((NSET, 128), jnp.float32)
        for j in range(CAND):
            value = value + jnp.where(codes[j : j + 1] == float(label), spread[j], 0.0)
        at = (label % CLS_DEV) * NSET
        coef_ref[label // CLS_DEV, at : at + NSET, :] = value.astype(jnp.bfloat16)


def softmax_call(row_index, parts, codes):
    vmem = pl.BlockSpec(memory_space=pltpu.VMEM)
    return pl.pallas_call(
        softmax_kernel,
        in_specs=[pl.BlockSpec(memory_space=pltpu.SMEM), vmem, vmem],
        out_specs=(vmem, vmem),
        out_shape=(
            jax.ShapeDtypeStruct((PART, CAND * ROT), jnp.float32),
            jax.ShapeDtypeStruct((COLS, CLS_DEV * NSET, 128), jnp.bfloat16),
        ),
        scratch_shapes=[pltpu.VMEM((128, 128), jnp.float32)],
        name="weights",
    )(row_index, parts, codes)


def sums_kernel(base_ref, coef_ref, *refs):
    pieces, class_ref, wedge_ref = refs[:-2], refs[-2], refs[-1]
    coefs = [coef_ref[base_ref[slot]] for slot in range(8)]
    start = 0
    for stop in (HALF, WIDTH):
        second = start > 0
        picks = ((0, 0), (1, 1), (2, 2), (3, 4 if second else 3))
        picks = picks + ((4, 5), (5, 6), (6, 7), (7, 9 if second else 8))
        total = None
        for slot, index in picks:
            ref = pieces[index]
            block = ref[:, start:stop] if ref.shape[1] == WIDTH else ref[...]
            term = jnp.dot(coefs[slot], block, preferred_element_type=jnp.float32)
            total = term if total is None else total + term
        if second:
            class_ref[:, start:] = total[:, : SLICE - start]
            at = SLICE + 128 - start
            wedge_ref[...] = total[:, at : at + 64]
        else:
            class_ref[:, :stop] = total
        start = stop


def sums_call(bases, coefs, pieces):
    vmem = pl.BlockSpec(memory_space=pltpu.VMEM)
    return pl.pallas_call(
        sums_kernel,
        in_specs=[pl.BlockSpec(memory_space=pltpu.SMEM)] + [vmem] * (1 + len(pieces)),
        out_specs=(vmem, vmem),
        out_shape=(
            jax.ShapeDtypeStruct((CLS_DEV * NSET, SLICE), jnp.float32),
            jax.ShapeDtypeStruct((CLS_DEV * NSET, 64), jnp.float32),
        ),
        name="sums",
    )(bases, coefs, *pieces)


def along_x(value, hops):
    pairs = [(i, ((i // 2 + hops) % 4) * 2 + i % 2) for i in range(COLS)]
    return lax.ppermute(value, "cls", pairs)


def other_core(value):
    return lax.ppermute(value, "cls", [(i, i ^ 1) for i in range(COLS)])


def around(value, first_half, second_half):
    ahead = along_x(value, 1)
    behind = along_x(value, -1)
    other = other_core(value)
    far_one = along_x(first_half(ahead), 1)
    far_two = along_x(second_half(behind), -1)
    other_near = [other_core(ahead), other_core(behind)]
    other_far = [other_core(far_one), other_core(far_two)]
    return [value, ahead, behind, far_one, far_two, other] + other_near + other_far


def inner(particles, inverse_noise, tomogram, candidates, rotations, wedge, references):
    row = lax.axis_index("tomo")
    col = lax.axis_index("cls")
    x, core = col >> 1, col & 1
    bases = jnp.stack(
        [((x + dx) & 3) * 2 + (core ^ k) for k in (0, 1) for dx in (0, 3, 1, 2)]
    ).astype(jnp.int32)

    flat_refs = references.reshape(CLS_DEV * NSET, 2 * KB**3)
    ref_slice = lax.dynamic_slice(flat_refs, (0, row * SLICE), (CLS_DEV * NSET, SLICE))
    ref_pieces = around(ref_slice, lambda v: v[:32], lambda v: v[32:])

    local = tomogram - row * wedge.shape[0]
    wedge_rows = wedge.reshape(wedge.shape[0], KB * KB)
    masks = jnp.zeros((PART, KB * KB), jnp.int32)
    for index in range(wedge.shape[0]):
        masks = jnp.where((local == index)[:, None], wedge_rows[index][None, :], masks)
    masks = masks.astype(jnp.float32)
    mask_tiles = jnp.tile(masks.reshape(PART, KB, KB).transpose(1, 0, 2), (1, 1, 4))
    planes = masks.reshape(PART, 8, 128).transpose(1, 0, 2)
    entries = masks.reshape(PART, ROWS, 64).transpose(1, 0, 2)
    codes = jnp.concatenate([candidates, rotations], axis=1).astype(jnp.float32)
    codes = jnp.pad(codes, ((0, 0), (0, 64 - CAND - ROT)))
    extras = jnp.concatenate(
        [
            jnp.concatenate([planes, planes], axis=0),
            entries,
            jnp.broadcast_to(codes[None], (ROWS, PART, 64)),
        ],
        axis=2,
    ).astype(jnp.bfloat16)
    spectra = spectra_call(particles, mask_tiles, extras)
    slots = lax.all_to_all(spectra, "tomo", 0, 0, tiled=True).reshape(ROWS * PART, WIDTH)
    slot_pieces = around(slots, lambda v: v[:, :HALF], lambda v: v[:, HALF:])

    lane = jnp.arange(128, dtype=jnp.int32)
    noise_row = jnp.where(lane // PART == row, jnp.tile(inverse_noise, ROWS), 0.0)
    noise_rows = jnp.broadcast_to(noise_row[None], (8, 128))
    partial, codes_turned = score_call(bases, slots, noise_rows, ref_pieces)
    copies = jnp.broadcast_to(partial[None], (ROWS,) + partial.shape)
    parts = lax.all_to_all(copies, "tomo", 0, 0, tiled=True)
    posterior, coefs = softmax_call(row.astype(jnp.int32)[None], parts, codes_turned)
    coefs = lax.all_to_all(coefs, "cls", 0, 0, tiled=True)
    class_sums, wedge_sums = sums_call(bases, coefs, slot_pieces)
    return (
        posterior,
        class_sums.reshape(CLS_DEV, NSET, SLICE),
        wedge_sums.reshape(CLS_DEV, NSET, 64),
    )


def solution(mesh):
    return jax.shard_map(
        inner,
        mesh=mesh,
        in_specs=(
            P(("tomo", "cls"), None, None),
            P(("tomo", "cls")),
            P(("tomo", "cls")),
            P(("tomo", "cls"), None),
            P(("tomo", "cls"), None),
            P("tomo", None, None),
            P("cls", None, None),
        ),
        out_specs=(P(("tomo", "cls"), None), P("cls", None, "tomo"), P("cls", None, "tomo")),
        check_vma=False,
    )
```

```python
import math

import jax
import jax.numpy as jnp
import numpy as np
from jax import lax
from jax.experimental import pallas as pl
from jax.experimental.pallas import tpu as pltpu
from jax.sharding import PartitionSpec as P


VOX = 64
KB = 32
NSET = 16
ROT = 8
CAND = 4
PART = 8
ROWS = 16
COLS = 8
CLS_DEV = 4
CLS_ROWS = CLS_DEV * NSET
SLICE = 2 * KB**3 // ROWS
HALF = SLICE // 2
WIDTH = HALF + 128
CODE_AT = 64
CHUNK = 1024


def split_table(table):
    high = table.astype(jnp.bfloat16)
    low = (table - np.asarray(high, np.float32)).astype(jnp.bfloat16)
    return high, low


def dft_constants(half):
    frequency = np.arange(KB) - KB // 2
    residue = (frequency[:, None] * np.arange(VOX)[None, :]) % VOX
    radians = residue * (2.0 * math.pi / VOX)
    both = (np.stack([np.cos(radians), -np.sin(radians)]) / math.sqrt(VOX)).astype(np.float32)
    depth_table = np.kron(np.eye(4, dtype=np.float32), both.reshape(2 * KB, VOX))
    wz = np.concatenate(split_table(depth_table), axis=0)
    kept = both.reshape(2, 8, 2, 2, VOX)[:, :, half].reshape(2, KB // 2, VOX)
    wide = np.einsum("akx,pq->pxakq", kept, np.eye(PART, dtype=np.float32))
    wxh, wxl = split_table(wide.reshape(PART * VOX, KB * PART))
    high, low = split_table(both.reshape(2 * KB, VOX))
    wy = np.concatenate([high, high, low], axis=1)
    return wz, wxh, wxl, wy


def mask_rows(tomo_ref, wedge_ref, cand_ref, rot_ref, index):
    table = wedge_ref[...].reshape(4 * KB, KB).astype(jnp.float32).astype(jnp.bfloat16)
    source = lax.broadcasted_iota(jnp.int32, (KB, 128), 0)
    lane = lax.broadcasted_iota(jnp.int32, (KB, 128), 1)
    wide = jnp.dot(
        table, ((lane & 31) == source).astype(jnp.bfloat16), preferred_element_type=jnp.float32
    ).astype(jnp.bfloat16)
    index[...] = jnp.zeros_like(index)
    index[:1, :PART] = tomo_ref[...].astype(jnp.float32)
    index[CODE_AT : CODE_AT + CAND, :PART] = cand_ref[...].astype(jnp.float32)
    turned = index[...].T[:PART]
    index[:PART, :] = turned
    index[:PART, CODE_AT + 8 : CODE_AT + 8 + ROT] = rot_ref[...].astype(jnp.float32)
    local = jnp.broadcast_to(turned[:, :1].astype(jnp.int32) & 3, (PART, 128))
    local = jnp.concatenate([local] * KB, axis=0)
    row = lax.broadcasted_iota(jnp.int32, (KB * PART, 128), 0)
    col = lax.broadcasted_iota(jnp.int32, (KB * PART, 128), 1)
    pick = (((col & 31) == (row >> 3)) & ((col >> 5) == local)).astype(jnp.bfloat16)
    return jnp.dot(pick, wide, preferred_element_type=jnp.float32)


def dft_kernel(
    half,
    p_ref,
    wz_ref,
    wxh_ref,
    wxl_ref,
    wy_ref,
    tomo_ref,
    wedge_ref,
    cand_ref,
    rot_ref,
    out_ref,
    mid,
    last,
    masks,
    index,
):
    step = pl.program_id(0)
    for block in range(CHUNK // 256):
        data = p_ref[:, :, block * 256 : (block + 1) * 256].reshape(PART * VOX, 256)
        first = lax.dot_general(
            wz_ref[...], data, (((1,), (1,)), ((), ())), preferred_element_type=jnp.float32
        )
        first = first[: 8 * KB] + first[8 * KB :]
        high = first.astype(jnp.bfloat16)
        low = (first - high.astype(jnp.float32)).astype(jnp.bfloat16)
        second = (
            jnp.dot(high, wxh_ref[...], preferred_element_type=jnp.float32)
            + jnp.dot(low, wxh_ref[...], preferred_element_type=jnp.float32)
            + jnp.dot(high, wxl_ref[...], preferred_element_type=jnp.float32)
        )
        for yy in range(4):
            cos_rows = second[yy * 64 : yy * 64 + 32]
            sin_rows = second[yy * 64 + 32 : yy * 64 + 64]
            at = (step * (CHUNK // 64) + block * 4 + yy) * KB
            rows = pl.ds(pl.multiple_of(at, KB), KB)
            mid[0, rows, :] = cos_rows[:, :128] - sin_rows[:, 128:]
            mid[1, rows, :] = sin_rows[:, :128] + cos_rows[:, 128:]

    @pl.when(step == pl.num_programs(0) - 1)
    def _():
        masks[...] = mask_rows(tomo_ref, wedge_ref, cand_ref, rot_ref, index)
        for kz in range(KB):
            values = jnp.concatenate(
                [mid[part, pl.ds(kz, VOX, stride=KB), :] for part in range(2)], axis=1
            )
            top = values.astype(jnp.bfloat16)
            rest = (values - top.astype(jnp.float32)).astype(jnp.bfloat16)
            third = jnp.dot(
                wy_ref[...],
                jnp.concatenate([top, rest, top], axis=0),
                preferred_element_type=jnp.float32,
            )
            rows = pl.ds(kz, KB, stride=KB)
            last[0, rows, :] = third[:KB, :128] - third[KB:, 128:]
            last[1, rows, :] = third[KB:, :128] + third[:KB, 128:]
        for part in range(2):
            turned = last[part].T
            for k in range(16):
                kx = (k // 2) * 4 + half * 2 + k % 2
                keep = jnp.concatenate([masks[kx * PART : (kx + 1) * PART, :]] * 8, axis=1)
                piece = turned[k * PART : (k + 1) * PART, :] * keep
                at = (k % 2) * 1024
                out_ref[part * 8 + k // 2, :, at : at + 1024] = piece.astype(jnp.bfloat16)
        lane = lax.broadcasted_iota(jnp.int32, (PART, 128), 1)
        table = lambda kx: masks[kx * PART : (kx + 1) * PART, :]
        if half == 0:
            for group in range(8):
                plane = jnp.zeros((PART, 128), jnp.float32)
                for k in range(4):
                    plane = jnp.where((lane >> 5) == k, table(group * 4 + k), plane)
                plane = plane.astype(jnp.bfloat16)
                out_ref[group, :, HALF:] = plane
                out_ref[group + 8, :, HALF:] = plane
        else:
            codes = index[:PART, :]
            for target in range(ROWS):
                entry = jnp.where(lane < KB, table(target * 2), table(target * 2 + 1))
                entry = jnp.where(lane < 2 * KB, entry, codes)
                out_ref[target, :, HALF:] = entry.astype(jnp.bfloat16)


def spectra_call(half, particles, tomogram, wedge, candidates, rotations):
    tables = dft_constants(half)
    small = (tomogram, wedge, candidates, rotations)
    whole = lambda array: pl.BlockSpec(array.shape, lambda i, n=array.ndim: (0,) * n)
    return pl.pallas_call(
        lambda *refs: dft_kernel(half, *refs),
        grid=(VOX * VOX // CHUNK,),
        in_specs=[pl.BlockSpec((PART, VOX, CHUNK), lambda i: (0, 0, i))]
        + [whole(array) for array in tables + small],
        out_specs=pl.BlockSpec((ROWS, PART, WIDTH), lambda i: (0, 0, 0)),
        out_shape=jax.ShapeDtypeStruct((ROWS, PART, WIDTH), jnp.bfloat16),
        scratch_shapes=[
            pltpu.VMEM((2, VOX * KB, 128), jnp.float32),
            pltpu.VMEM((2, KB * KB, 128), jnp.float32),
            pltpu.VMEM((KB * PART, 128), jnp.float32),
            pltpu.VMEM((128, 128), jnp.float32),
        ],
        compiler_params=pltpu.CompilerParams(dimension_semantics=("arbitrary",)),
        cost_estimate=pl.CostEstimate(
            flops=10_000_000_000, bytes_accessed=6_000_000, transcendentals=0
        ),
    )(particles, *(jnp.asarray(table) for table in tables), *small)


CONTRACT = (((1,), (1,)), ((), ()))


def cls_of(col, index):
    x = ((col >> 1) + (0, 3, 1, 2)[index % 4]) & 3
    return (x << 1) + ((col & 1) ^ (index // 4))


def stacked_pieces(refs):
    return jnp.concatenate([ref[...] for ref in refs], axis=0)


def score_first_kernel(slots_ref, plane_ref, *refs):
    pieces, out_ref = refs[:-1], refs[-1]
    step = pl.program_id(0)
    values = stacked_pieces(pieces)
    row = lax.broadcasted_iota(jnp.int32, (128, 128), 0)
    col = lax.broadcasted_iota(jnp.int32, (128, 128), 1)
    term = None
    for k in range(2):
        spread = ((row >> 5) == 2 * step + k) & ((row & 31) == (col & 31))
        keep = jnp.dot(
            plane_ref[...], spread.astype(jnp.bfloat16), preferred_element_type=jnp.float32
        ).astype(jnp.bfloat16)
        power = jnp.zeros((COLS * CLS_ROWS, 128), jnp.float32)
        for j in range(8):
            at = k * 1024 + j * 128
            value = values[:, at : at + 128].astype(jnp.float32)
            power = power + value * value
        one = power.astype(jnp.bfloat16)
        left = power - one.astype(jnp.float32)
        two = left.astype(jnp.bfloat16)
        three = (left - two.astype(jnp.float32)).astype(jnp.bfloat16)
        for part in (three, two, one):
            more = lax.dot_general(part, keep, CONTRACT, preferred_element_type=jnp.float32)
            term = more if term is None else term + more

    @pl.when(step == 0)
    def _():
        out_ref[...] = -0.5 * term + lax.dot_general(
            values, slots_ref[...], CONTRACT, preferred_element_type=jnp.float32
        )

    @pl.when(step == 1)
    def _():
        out_ref[...] += -0.5 * term


def score_first_call(slots, pieces):
    return pl.pallas_call(
        score_first_kernel,
        grid=(2,),
        in_specs=[
            pl.BlockSpec((128, HALF), lambda i: (0, 0)),
            pl.BlockSpec((128, 128), lambda i: (0, HALF // 128)),
        ]
        + [pl.BlockSpec((CLS_ROWS, HALF), lambda i: (0, i))] * COLS,
        out_specs=pl.BlockSpec((COLS * CLS_ROWS, 128), lambda i: (0, 0)),
        out_shape=jax.ShapeDtypeStruct((COLS * CLS_ROWS, 128), jnp.float32),
        compiler_params=pltpu.CompilerParams(dimension_semantics=("arbitrary",)),
        cost_estimate=pl.CostEstimate(
            flops=1_000_000_000, bytes_accessed=5_000_000, transcendentals=0
        ),
        name="score0",
    )(slots, slots, *pieces)


def score_second_kernel(col_ref, slots_ref, code_ref, noise_ref, begun_ref, *refs):
    pieces, out_ref, codes_ref, table = refs[:COLS], refs[-3], refs[-2], refs[-1]
    step = pl.program_id(0)
    inner = lax.dot_general(
        stacked_pieces(pieces), slots_ref[...], CONTRACT, preferred_element_type=jnp.float32
    )

    @pl.when(step == 0)
    def _():
        table[...] = begun_ref[...] + inner

    @pl.when(step == 1)
    def _():
        table[...] += inner
        codes = code_ref[...].astype(jnp.float32).T[CODE_AT : CODE_AT + 16]
        codes_ref[...] = codes
        chosen = [jnp.zeros((NSET, 128), jnp.float32) for _ in range(CAND)]
        for index in range(COLS):
            first = cls_of(col_ref[0], index) * CLS_DEV
            for local in range(CLS_DEV):
                label = (first + local).astype(jnp.float32)
                at = index * CLS_ROWS + local * NSET
                block = table[at : at + NSET]
                for j in range(CAND):
                    chosen[j] = chosen[j] + jnp.where(codes[j : j + 1] == label, block, 0.0)
        copies = lax.broadcasted_iota(jnp.int32, (NSET, 128), 0).astype(jnp.float32)
        for r in range(ROT):
            hit = codes[8 + r : 9 + r] == copies
            for j in range(CAND):
                value = jnp.sum(jnp.where(hit, chosen[j], 0.0), axis=0, keepdims=True)
                out_ref[0, j * ROT + r : j * ROT + r + 1, :] = value
        out_ref[0, CAND * ROT :, :] = jnp.zeros((8, 128), jnp.float32)
        out_ref[0, CAND * ROT : CAND * ROT + 1, :PART] = noise_ref[...]
        whole = out_ref[0]
        for target in range(1, ROWS):
            out_ref[target] = whole


def score_second_call(col, slots, noise, begun, pieces):
    return pl.pallas_call(
        score_second_kernel,
        grid=(2,),
        in_specs=[
            pl.BlockSpec(memory_space=pltpu.SMEM),
            pl.BlockSpec((128, 1024), lambda i: (0, i)),
            pl.BlockSpec((128, 128), lambda i: (0, HALF // 128)),
            pl.BlockSpec((1, PART), lambda i: (0, 0)),
            pl.BlockSpec((COLS * CLS_ROWS, 128), lambda i: (0, 0)),
        ]
        + [pl.BlockSpec((CLS_ROWS, 1024), lambda i: (0, 2 + i))] * COLS,
        out_specs=(
            pl.BlockSpec((ROWS, CAND * ROT + 8, 128), lambda i: (0, 0, 0)),
            pl.BlockSpec((16, 128), lambda i: (0, 0)),
        ),
        out_shape=(
            jax.ShapeDtypeStruct((ROWS, CAND * ROT + 8, 128), jnp.float32),
            jax.ShapeDtypeStruct((16, 128), jnp.float32),
        ),
        scratch_shapes=[pltpu.VMEM((COLS * CLS_ROWS, 128), jnp.float32)],
        compiler_params=pltpu.CompilerParams(dimension_semantics=("arbitrary",)),
        cost_estimate=pl.CostEstimate(
            flops=1_000_000_000, bytes_accessed=4_000_000, transcendentals=0
        ),
        name="score1",
    )(col, slots, slots, noise, begun, *pieces)


def softmax_kernel(at_ref, parts_ref, codes_ref, post_ref, coef_ref, turned):
    total = parts_ref[0, : CAND * ROT]
    noise = parts_ref[0, CAND * ROT :]
    for row in range(1, ROWS):
        total = total + parts_ref[row, : CAND * ROT]
        noise = noise + pltpu.roll(parts_ref[row, CAND * ROT :], row * PART, 1)
    logits = noise[:1] * total
    peak = jnp.max(logits, axis=0, keepdims=True)
    weight = jnp.exp(logits - peak)
    posterior = weight / jnp.sum(weight, axis=0, keepdims=True)
    padded = jnp.concatenate([posterior, jnp.zeros((96, 128), jnp.float32)], axis=0)
    turned[...] = padded.T
    own = turned[pl.ds(pl.multiple_of(at_ref[0] * PART, PART), PART), :]
    post_ref[...] = own[:, : CAND * ROT]
    rounded = posterior.astype(jnp.bfloat16).astype(jnp.float32)
    codes = codes_ref[...]
    copies = lax.broadcasted_iota(jnp.int32, (NSET, 128), 0).astype(jnp.float32)
    spread = []
    for j in range(CAND):
        value = jnp.zeros((NSET, 128), jnp.float32)
        for r in range(ROT):
            hit = codes[8 + r : 9 + r] == copies
            value = value + jnp.where(hit, rounded[j * ROT + r : j * ROT + r + 1], 0.0)
        spread.append(value)
    for label in range(COLS * CLS_DEV):
        value = jnp.zeros((NSET, 128), jnp.float32)
        for j in range(CAND):
            value = value + jnp.where(codes[j : j + 1] == float(label), spread[j], 0.0)
        at = (label % CLS_DEV) * NSET
        coef_ref[label // CLS_DEV, at : at + NSET, :] = value.astype(jnp.bfloat16)


def softmax_call(row_index, parts, codes):
    vmem = pl.BlockSpec(memory_space=pltpu.VMEM)
    return pl.pallas_call(
        softmax_kernel,
        in_specs=[pl.BlockSpec(memory_space=pltpu.SMEM), vmem, vmem],
        out_specs=(vmem, vmem),
        out_shape=(
            jax.ShapeDtypeStruct((PART, CAND * ROT), jnp.float32),
            jax.ShapeDtypeStruct((COLS, CLS_DEV * NSET, 128), jnp.bfloat16),
        ),
        scratch_shapes=[pltpu.VMEM((128, 128), jnp.float32)],
        name="weights",
    )(row_index, parts, codes)


def sums_kernel(half, col_ref, coef_ref, *refs):
    pieces = refs[:COLS]
    coefs = [coef_ref[cls_of(col_ref[0], slot)] for slot in range(COLS)]

    def combine(blocks):
        total = None
        for coef, ref in zip(coefs, blocks):
            term = jnp.dot(coef, ref[...], preferred_element_type=jnp.float32)
            total = term if total is None else total + term
        return total

    if half == 0:
        refs[COLS][...] = combine(pieces)
        return
    class_ref, wedge_ref = refs[-2], refs[-1]
    class_ref[...] = combine(pieces)

    @pl.when(pl.program_id(0) == 0)
    def _():
        wedge_ref[...] = combine(refs[COLS : 2 * COLS])[:, :64]


def sums_call(half, col, coefs, pieces, begun=None):
    block = HALF // 2
    spec = pl.BlockSpec((128, block), lambda i: (0, i))
    in_specs = [
        pl.BlockSpec(memory_space=pltpu.SMEM),
        pl.BlockSpec((COLS, CLS_ROWS, 128), lambda i: (0, 0, 0)),
    ] + [spec] * COLS
    operands = [col, coefs] + list(pieces)
    out_specs = [pl.BlockSpec((CLS_ROWS, block), lambda i: (0, 2 * half + i))]
    out_shape = [jax.ShapeDtypeStruct((CLS_ROWS, SLICE), jnp.float32)]
    aliases = {}
    if half == 1:
        in_specs += [pl.BlockSpec((128, 128), lambda i: (0, HALF // 128))] * COLS
        operands += list(pieces)
        aliases = {len(operands): 0}
        in_specs.append(pl.BlockSpec(memory_space=pl.ANY))
        operands.append(begun)
        out_specs.append(pl.BlockSpec((CLS_ROWS, 64), lambda i: (0, 0)))
        out_shape.append(jax.ShapeDtypeStruct((CLS_ROWS, 64), jnp.float32))
    return pl.pallas_call(
        lambda *refs: sums_kernel(half, *refs),
        grid=(2,),
        in_specs=in_specs,
        out_specs=out_specs,
        out_shape=out_shape,
        input_output_aliases=aliases,
        compiler_params=pltpu.CompilerParams(dimension_semantics=("arbitrary",)),
        cost_estimate=pl.CostEstimate(
            flops=300_000_000, bytes_accessed=5_000_000, transcendentals=0
        ),
    )(*operands)


def along_x(value, hops):
    pairs = [(i, ((i // 2 + hops) % 4) * 2 + i % 2) for i in range(COLS)]
    return lax.ppermute(value, "cls", pairs)


def other_core(value):
    return lax.ppermute(value, "cls", [(i, i ^ 1) for i in range(COLS)])


def around(value, forward):
    ahead = along_x(value, 1)
    behind = along_x(value, -1)
    other = other_core(value)
    far = along_x(ahead, 1) if forward else along_x(behind, -1)
    other_near = [other_core(ahead), other_core(behind)]
    other_far = other_core(far)
    return [value, ahead, behind, far, other] + other_near + [other_far]


def inner(particles, inverse_noise, tomogram, candidates, rotations, wedge, references):
    row = lax.axis_index("tomo")
    col = lax.axis_index("cls")
    row_ref = row.astype(jnp.int32)[None]
    col_ref = col.astype(jnp.int32)[None]

    flat_refs = references.reshape(CLS_ROWS, 2 * KB**3)
    ref_slice = lax.dynamic_slice(flat_refs, (0, row * SLICE), (CLS_ROWS, SLICE))
    ref_pieces = around(ref_slice, True)

    small = (tomogram[None], wedge, candidates.T, rotations)
    slots, slot_pieces = [], []
    for half in (0, 1):
        spectra = spectra_call(half, particles, *small)
        moved = lax.all_to_all(spectra, "tomo", 0, 0, tiled=True)
        slots.append(moved.reshape(ROWS * PART, WIDTH))
        slot_pieces.append(around(slots[half], half == 0))

    begun = score_first_call(slots[0], ref_pieces)
    copies, codes = score_second_call(
        col_ref, slots[1], inverse_noise[None], begun, ref_pieces
    )
    parts = lax.all_to_all(copies, "tomo", 0, 0, tiled=True)
    posterior, coefs = softmax_call(row_ref, parts, codes)
    coefs = lax.all_to_all(coefs, "cls", 0, 0, tiled=True)
    (class_sums,) = sums_call(0, col_ref, coefs, slot_pieces[0])
    class_sums, wedge_sums = sums_call(1, col_ref, coefs, slot_pieces[1], class_sums)
    return (
        posterior,
        class_sums.reshape(CLS_DEV, NSET, SLICE),
        wedge_sums.reshape(CLS_DEV, NSET, 64),
    )


def solution(mesh):
    return jax.shard_map(
        inner,
        mesh=mesh,
        in_specs=(
            P(("tomo", "cls"), None, None),
            P(("tomo", "cls")),
            P(("tomo", "cls")),
            P(("tomo", "cls"), None),
            P(("tomo", "cls"), None),
            P("tomo", None, None),
            P("cls", None, None),
        ),
        out_specs=(P(("tomo", "cls"), None), P("cls", None, "tomo"), P("cls", None, "tomo")),
        check_vma=False,
    )
```

```python
import math

import jax
import jax.numpy as jnp
import numpy as np
from jax import lax
from jax.experimental import pallas as pl
from jax.experimental.pallas import tpu as pltpu
from jax.sharding import PartitionSpec as P


VOX = 64
KB = 32
NSET = 16
ROT = 8
CAND = 4
PART = 8
ROWS = 16
COLS = 8
CLS_DEV = 4
CLS_ROWS = CLS_DEV * NSET
SLICE = 2 * KB**3 // ROWS
HALF = SLICE // 2
WIDTH = HALF + 128
CODE_AT = 64
CHUNK = 1024


def split_table(table):
    high = table.astype(jnp.bfloat16)
    low = (table - np.asarray(high, np.float32)).astype(jnp.bfloat16)
    return high, low


def dft_constants():
    frequency = np.arange(KB) - KB // 2
    residue = (frequency[:, None] * np.arange(VOX)[None, :]) % VOX
    radians = residue * (2.0 * math.pi / VOX)
    both = (np.stack([np.cos(radians), -np.sin(radians)]) / math.sqrt(VOX)).astype(np.float32)
    one = lambda size: np.eye(size, dtype=np.float32)
    depth = np.einsum("ckz,yv->ckyvz", both, one(4)).reshape(8 * KB, 4 * VOX)
    wz = np.concatenate(split_table(depth), axis=0)
    kept = both.reshape(2, 8, 2, 2, VOX).transpose(0, 2, 1, 3, 4).reshape(2, 2, 16, VOX)
    wide = np.einsum("ahkx,pq->pxahkq", kept, one(4)).reshape(4 * VOX, 8 * KB)
    wxh, wxl = split_table(wide)
    tall = np.einsum("ckbv,eu->ckebuv", both.reshape(2, KB, 16, 4), one(2))
    high, low = split_table(tall.reshape(4 * KB, 2 * VOX))
    wy = np.concatenate([high, high, low], axis=1)
    order = np.einsum("ij,kl,mn->ikmljn", one(8), one(16), one(2))
    order = order.reshape(256, 256).astype(jnp.bfloat16)
    turn = np.einsum("ab,gh,kl,pq->akgpbhlq", one(2), one(2), one(16), one(4))
    turn = turn.reshape(256, 256).astype(jnp.bfloat16)
    return (wz, wxh, wxl), (wy, order, turn)


CONTRACT = (((1,), (1,)), ((), ()))


def mask_rows(tomo_ref, wedge_ref, cand_ref, rot_ref, index):
    table = wedge_ref[...].reshape(4 * KB, KB).astype(jnp.float32).astype(jnp.bfloat16)
    source = lax.broadcasted_iota(jnp.int32, (KB, 128), 0)
    lane = lax.broadcasted_iota(jnp.int32, (KB, 128), 1)
    wide = jnp.dot(
        table, ((lane & 31) == source).astype(jnp.bfloat16), preferred_element_type=jnp.float32
    ).astype(jnp.bfloat16)
    index[...] = jnp.zeros_like(index)
    index[:1, :PART] = tomo_ref[...].astype(jnp.float32)
    index[CODE_AT : CODE_AT + CAND, :PART] = cand_ref[...].astype(jnp.float32)
    turned = index[...].T[:PART]
    index[:PART, :] = turned
    index[:PART, CODE_AT + 8 : CODE_AT + 8 + ROT] = rot_ref[...].astype(jnp.float32)
    local = jnp.broadcast_to(turned[:, :1].astype(jnp.int32) & 3, (PART, 128))
    local = jnp.concatenate([local] * KB, axis=0)
    row = lax.broadcasted_iota(jnp.int32, (KB * PART, 128), 0)
    col = lax.broadcasted_iota(jnp.int32, (KB * PART, 128), 1)
    pick = (((col & 31) == (row >> 3)) & ((col >> 5) == local)).astype(jnp.bfloat16)
    return jnp.dot(pick, wide, preferred_element_type=jnp.float32)


def dft_tail(half, mid, tail_refs, out_ref, last, masks, index):
    wy_ref, order_ref, turn_ref, tomo_ref, wedge_ref, cand_ref, rot_ref = tail_refs
    masks[...] = mask_rows(tomo_ref, wedge_ref, cand_ref, rot_ref, index)
    for pair in range(16):
        values = jnp.concatenate([mid[0, pair], mid[1, pair]], axis=1)
        top = values.astype(jnp.bfloat16)
        rest = (values - top.astype(jnp.float32)).astype(jnp.bfloat16)
        third = jnp.dot(
            wy_ref[...],
            jnp.concatenate([top, rest, top], axis=0),
            preferred_element_type=jnp.float32,
        )
        real = third[: 2 * KB, :128] - third[2 * KB :, 128:]
        imag = third[2 * KB :, :128] + third[: 2 * KB, 128:]
        last[pair] = jnp.concatenate([real, imag], axis=1).astype(jnp.bfloat16)
    for group in range(4):
        rows = slice(group * 16, (group + 1) * 16)
        chunk = jnp.concatenate([last[pair, rows, :] for pair in range(16)], axis=0)
        ordered = jnp.dot(order_ref[...], chunk, preferred_element_type=jnp.float32)
        turned = lax.dot_general(
            turn_ref[...],
            ordered.astype(jnp.bfloat16),
            CONTRACT,
            preferred_element_type=jnp.float32,
        )
        for part in range(2):
            for k in range(16):
                kx = (k // 2) * 4 + half * 2 + k % 2
                keep = masks[kx * PART : (kx + 1) * PART, :]
                at = part * 128 + k * PART
                piece = turned[at : at + PART, :] * jnp.concatenate([keep, keep], axis=1)
                at = (k % 2) * 1024 + group * 256
                out_ref[part * 8 + k // 2, :, at : at + 256] = piece.astype(jnp.bfloat16)
    lane = lax.broadcasted_iota(jnp.int32, (PART, 128), 1)
    table = lambda kx: masks[kx * PART : (kx + 1) * PART, :]
    if half == 0:
        for group in range(8):
            plane = jnp.zeros((PART, 128), jnp.float32)
            for k in range(4):
                plane = jnp.where((lane >> 5) == k, table(group * 4 + k), plane)
            plane = plane.astype(jnp.bfloat16)
            out_ref[group, :, HALF:] = plane
            out_ref[group + 8, :, HALF:] = plane
    else:
        codes = index[:PART, :]
        for target in range(ROWS):
            entry = jnp.where(lane < KB, table(target * 2), table(target * 2 + 1))
            entry = jnp.where(lane < 2 * KB, entry, codes)
            out_ref[target, :, HALF:] = entry.astype(jnp.bfloat16)


def dft_kernel(p_ref, wz_ref, wxh_ref, wxl_ref, *refs):
    tail_refs = refs[:7]
    out_ref, later_ref, mid, last, masks, index = refs[7:]
    step = pl.program_id(0)
    lane = lax.broadcasted_iota(jnp.int32, (128, 128), 1)
    for block in range(CHUNK // 256):
        data = p_ref[:, :, block * 256 : (block + 1) * 256].reshape(PART * VOX, 256)
        first = lax.dot_general(
            wz_ref[...], data, CONTRACT, preferred_element_type=jnp.float32
        )
        first = first[: 8 * KB] + first[8 * KB :]
        first = jnp.concatenate([first[:, :256], first[:, 256:]], axis=0)
        high = first.astype(jnp.bfloat16)
        low = (first - high.astype(jnp.float32)).astype(jnp.bfloat16)
        second = (
            jnp.dot(high, wxh_ref[...], preferred_element_type=jnp.float32)
            + jnp.dot(low, wxh_ref[...], preferred_element_type=jnp.float32)
            + jnp.dot(high, wxl_ref[...], preferred_element_type=jnp.float32)
        )
        cos_rows = [second[:128], second[256:384]]
        sin_rows = [second[128:256], second[384:]]
        real = [c[:, :128] - s[:, 128:] for c, s in zip(cos_rows, sin_rows)]
        imag = [s[:, :128] + c[:, 128:] for c, s in zip(cos_rows, sin_rows)]
        at = pl.multiple_of((step * (CHUNK // 256) + block) * 8, 8)
        for part, (one, two) in enumerate((real, imag)):
            left = jnp.where(lane < 64, one, pltpu.roll(two, 64, 1))
            right = jnp.where(lane < 64, pltpu.roll(one, 64, 1), two)
            mid[part, :, pl.ds(at, 8), :] = left.reshape(16, 8, 128)
            later_ref[part, :, block * 8 : (block + 1) * 8, :] = right.reshape(16, 8, 128)

    @pl.when(step == pl.num_programs(0) - 1)
    def _():
        dft_tail(0, mid, tail_refs, out_ref, last, masks, index)


def tail_kernel(mid_ref, *refs):
    out_ref, last, masks, index = refs[7:]
    dft_tail(1, mid_ref, refs[:7], out_ref, last, masks, index)


TAIL_SCRATCH = (
    pltpu.VMEM((16, 2 * KB, 256), jnp.bfloat16),
    pltpu.VMEM((KB * PART, 128), jnp.float32),
    pltpu.VMEM((128, 128), jnp.float32),
)


def first_half_call(particles, front, tail):
    whole = lambda array: pl.BlockSpec(array.shape, lambda i, n=array.ndim: (0,) * n)
    steps = VOX * VOX // CHUNK
    return pl.pallas_call(
        dft_kernel,
        grid=(steps,),
        in_specs=[pl.BlockSpec((PART, VOX, CHUNK), lambda i: (0, 0, i))]
        + [whole(array) for array in front + tail],
        out_specs=(
            pl.BlockSpec((ROWS, PART, WIDTH), lambda i: (0, 0, 0)),
            pl.BlockSpec((2, 16, 128 // steps, 128), lambda i: (0, 0, i, 0)),
        ),
        out_shape=(
            jax.ShapeDtypeStruct((ROWS, PART, WIDTH), jnp.bfloat16),
            jax.ShapeDtypeStruct((2, 16, 128, 128), jnp.float32),
        ),
        scratch_shapes=(pltpu.VMEM((2, 16, 128, 128), jnp.float32),) + TAIL_SCRATCH,
        compiler_params=pltpu.CompilerParams(dimension_semantics=("arbitrary",)),
        cost_estimate=pl.CostEstimate(
            flops=10_000_000_000, bytes_accessed=8_000_000, transcendentals=0
        ),
        name="dft0",
    )(particles, *front, *tail)


def second_half_call(mid, tail):
    vmem = pl.BlockSpec(memory_space=pltpu.VMEM)
    return pl.pallas_call(
        tail_kernel,
        in_specs=[vmem] * (1 + len(tail)),
        out_specs=vmem,
        out_shape=jax.ShapeDtypeStruct((ROWS, PART, WIDTH), jnp.bfloat16),
        scratch_shapes=TAIL_SCRATCH,
        cost_estimate=pl.CostEstimate(
            flops=2_000_000_000, bytes_accessed=4_000_000, transcendentals=0
        ),
        name="dft1",
    )(mid, *tail)


def cls_of(col, index):
    x = ((col >> 1) + (0, 3, 1, 2)[index % 4]) & 3
    return (x << 1) + ((col & 1) ^ (index // 4))


def score_first_kernel(slots_ref, *refs):
    pieces, out_ref = refs[:-1], refs[-1]
    row = lax.broadcasted_iota(jnp.int32, (128, 128), 0)
    col = lax.broadcasted_iota(jnp.int32, (128, 128), 1)
    term = None
    for k in range(4):
        spread = ((row >> 5) == k) & ((row & 31) == (col & 31))
        keep = jnp.dot(
            slots_ref[:, HALF:], spread.astype(jnp.bfloat16), preferred_element_type=jnp.float32
        ).astype(jnp.bfloat16)
        sums = []
        for ref in pieces:
            power = jnp.zeros((CLS_ROWS, 128), jnp.float32)
            for j in range(8):
                at = k * 1024 + j * 128
                value = ref[:, at : at + 128].astype(jnp.float32)
                power = power + value * value
            sums.append(power)
        power = jnp.concatenate(sums, axis=0)
        one = power.astype(jnp.bfloat16)
        left = power - one.astype(jnp.float32)
        two = left.astype(jnp.bfloat16)
        three = (left - two.astype(jnp.float32)).astype(jnp.bfloat16)
        for part in (three, two, one):
            more = lax.dot_general(part, keep, CONTRACT, preferred_element_type=jnp.float32)
            term = more if term is None else term + more
    values = jnp.concatenate([ref[:, :HALF] for ref in pieces], axis=0)
    out_ref[...] = -0.5 * term + lax.dot_general(
        values, slots_ref[:, :HALF], CONTRACT, preferred_element_type=jnp.float32
    )


def score_first_call(slots, pieces):
    vmem = pl.BlockSpec(memory_space=pltpu.VMEM)
    return pl.pallas_call(
        score_first_kernel,
        in_specs=[vmem] * (1 + COLS),
        out_specs=vmem,
        out_shape=jax.ShapeDtypeStruct((COLS * CLS_ROWS, 128), jnp.float32),
        compiler_params=pltpu.CompilerParams(vmem_limit_bytes=32 << 20),
        cost_estimate=pl.CostEstimate(
            flops=1_000_000_000, bytes_accessed=5_000_000, transcendentals=0
        ),
        name="score0",
    )(slots, *pieces)


def score_second_kernel(col_ref, slots_ref, noise_ref, begun_ref, *refs):
    pieces, out_ref, codes_ref = refs[:COLS], refs[-2], refs[-1]
    values = jnp.concatenate([ref[:, HALF:] for ref in pieces], axis=0)
    table = begun_ref[...] + lax.dot_general(
        values, slots_ref[:, :HALF], CONTRACT, preferred_element_type=jnp.float32
    )
    codes = slots_ref[:, HALF:].astype(jnp.float32).T[CODE_AT : CODE_AT + 16]
    codes_ref[...] = codes
    chosen = [jnp.zeros((NSET, 128), jnp.float32) for _ in range(CAND)]
    for index in range(COLS):
        first = cls_of(col_ref[0], index) * CLS_DEV
        for local in range(CLS_DEV):
            label = (first + local).astype(jnp.float32)
            at = index * CLS_ROWS + local * NSET
            block = table[at : at + NSET]
            for j in range(CAND):
                chosen[j] = chosen[j] + jnp.where(codes[j : j + 1] == label, block, 0.0)
    copies = lax.broadcasted_iota(jnp.int32, (NSET, 128), 0).astype(jnp.float32)
    for r in range(ROT):
        hit = codes[8 + r : 9 + r] == copies
        for j in range(CAND):
            value = jnp.sum(jnp.where(hit, chosen[j], 0.0), axis=0, keepdims=True)
            out_ref[0, j * ROT + r : j * ROT + r + 1, :] = value
    out_ref[0, CAND * ROT :, :] = jnp.zeros((8, 128), jnp.float32)
    out_ref[0, CAND * ROT : CAND * ROT + 1, :PART] = noise_ref[...]
    whole = out_ref[0]
    for target in range(1, ROWS):
        out_ref[target] = whole


def score_second_call(col, slots, noise, begun, pieces):
    vmem = pl.BlockSpec(memory_space=pltpu.VMEM)
    return pl.pallas_call(
        score_second_kernel,
        in_specs=[pl.BlockSpec(memory_space=pltpu.SMEM)] + [vmem] * (3 + COLS),
        out_specs=(vmem, vmem),
        out_shape=(
            jax.ShapeDtypeStruct((ROWS, CAND * ROT + 8, 128), jnp.float32),
            jax.ShapeDtypeStruct((16, 128), jnp.float32),
        ),
        compiler_params=pltpu.CompilerParams(vmem_limit_bytes=32 << 20),
        cost_estimate=pl.CostEstimate(
            flops=1_000_000_000, bytes_accessed=4_000_000, transcendentals=0
        ),
        name="score1",
    )(col, slots, noise, begun, *pieces)


def softmax_kernel(at_ref, parts_ref, codes_ref, post_ref, coef_ref, turned):
    total = parts_ref[0, : CAND * ROT]
    noise = parts_ref[0, CAND * ROT :]
    for row in range(1, ROWS):
        total = total + parts_ref[row, : CAND * ROT]
        noise = noise + pltpu.roll(parts_ref[row, CAND * ROT :], row * PART, 1)
    logits = noise[:1] * total
    peak = jnp.max(logits, axis=0, keepdims=True)
    weight = jnp.exp(logits - peak)
    posterior = weight / jnp.sum(weight, axis=0, keepdims=True)
    padded = jnp.concatenate([posterior, jnp.zeros((96, 128), jnp.float32)], axis=0)
    turned[...] = padded.T
    own = turned[pl.ds(pl.multiple_of(at_ref[0] * PART, PART), PART), :]
    post_ref[...] = own[:, : CAND * ROT]
    rounded = posterior.astype(jnp.bfloat16).astype(jnp.float32)
    codes = codes_ref[...]
    copies = lax.broadcasted_iota(jnp.int32, (NSET, 128), 0).astype(jnp.float32)
    spread = []
    for j in range(CAND):
        value = jnp.zeros((NSET, 128), jnp.float32)
        for r in range(ROT):
            hit = codes[8 + r : 9 + r] == copies
            value = value + jnp.where(hit, rounded[j * ROT + r : j * ROT + r + 1], 0.0)
        spread.append(value)
    for label in range(COLS * CLS_DEV):
        value = jnp.zeros((NSET, 128), jnp.float32)
        for j in range(CAND):
            value = value + jnp.where(codes[j : j + 1] == float(label), spread[j], 0.0)
        at = (label % CLS_DEV) * NSET
        coef_ref[label // CLS_DEV, at : at + NSET, :] = value.astype(jnp.bfloat16)


def softmax_call(row_index, parts, codes):
    vmem = pl.BlockSpec(memory_space=pltpu.VMEM)
    return pl.pallas_call(
        softmax_kernel,
        in_specs=[pl.BlockSpec(memory_space=pltpu.SMEM), vmem, vmem],
        out_specs=(vmem, vmem),
        out_shape=(
            jax.ShapeDtypeStruct((PART, CAND * ROT), jnp.float32),
            jax.ShapeDtypeStruct((COLS, CLS_DEV * NSET, 128), jnp.bfloat16),
        ),
        scratch_shapes=[pltpu.VMEM((128, 128), jnp.float32)],
        compiler_params=pltpu.CompilerParams(vmem_limit_bytes=4 << 20),
        name="weights",
    )(row_index, parts, codes)


def sums_kernel(col_ref, coef_ref, *refs):
    pieces, class_ref, wedge_ref = refs[:-2], refs[-2], refs[-1]
    coefs = [coef_ref[cls_of(col_ref[0], slot)] for slot in range(COLS)]

    def combine(half, start, stop):
        total = None
        for coef, ref in zip(coefs, pieces[half * COLS : (half + 1) * COLS]):
            term = jnp.dot(coef, ref[:, start:stop], preferred_element_type=jnp.float32)
            total = term if total is None else total + term
        return total

    for half in range(2):
        for start in range(0, HALF, 512):
            at = half * HALF + start
            class_ref[:, at : at + 512] = combine(half, start, start + 512)
    wedge_ref[...] = combine(1, HALF, WIDTH)[:, :64]


def sums_call(col, coefs, pieces):
    vmem = pl.BlockSpec(memory_space=pltpu.VMEM)
    return pl.pallas_call(
        sums_kernel,
        in_specs=[pl.BlockSpec(memory_space=pltpu.SMEM)] + [vmem] * (1 + 2 * COLS),
        out_specs=(vmem, vmem),
        out_shape=(
            jax.ShapeDtypeStruct((CLS_ROWS, SLICE), jnp.float32),
            jax.ShapeDtypeStruct((CLS_ROWS, 64), jnp.float32),
        ),
        compiler_params=pltpu.CompilerParams(vmem_limit_bytes=16 << 20),
        cost_estimate=pl.CostEstimate(
            flops=600_000_000, bytes_accessed=10_000_000, transcendentals=0
        ),
        name="sums",
    )(col, coefs, *pieces)


def along_x(value, hops):
    pairs = [(i, ((i // 2 + hops) % 4) * 2 + i % 2) for i in range(COLS)]
    return lax.ppermute(value, "cls", pairs)


def other_core(value):
    return lax.ppermute(value, "cls", [(i, i ^ 1) for i in range(COLS)])


def around(value, forward):
    ahead = along_x(value, 1)
    behind = along_x(value, -1)
    other = other_core(value)
    far = along_x(ahead, 1) if forward else along_x(behind, -1)
    other_near = [other_core(ahead), other_core(behind)]
    other_far = other_core(far)
    return [value, ahead, behind, far, other] + other_near + [other_far]


def inner(particles, inverse_noise, tomogram, candidates, rotations, wedge, references):
    row = lax.axis_index("tomo")
    col = lax.axis_index("cls")
    row_ref = row.astype(jnp.int32)[None]
    col_ref = col.astype(jnp.int32)[None]

    flat_refs = references.reshape(CLS_ROWS, 2 * KB**3)
    ref_slice = lax.dynamic_slice(flat_refs, (0, row * SLICE), (CLS_ROWS, SLICE))
    ref_pieces = around(ref_slice, True)

    small = (tomogram[None], wedge, candidates.T, rotations)
    front, tail = dft_constants()
    front = tuple(jnp.asarray(table) for table in front)
    tail = tuple(jnp.asarray(table) for table in tail) + small
    first_half, later = first_half_call(particles, front, tail)
    second_half = second_half_call(later, tail)
    slots, slot_pieces = [], []
    for half, spectra in enumerate((first_half, second_half)):
        moved = lax.all_to_all(spectra, "tomo", 0, 0, tiled=True)
        slots.append(moved.reshape(ROWS * PART, WIDTH))
        slot_pieces.append(around(slots[half], half == 0))

    begun = score_first_call(slots[0], ref_pieces)
    copies, codes = score_second_call(
        col_ref, slots[1], inverse_noise[None], begun, ref_pieces
    )
    parts = lax.all_to_all(copies, "tomo", 0, 0, tiled=True)
    posterior, coefs = softmax_call(row_ref, parts, codes)
    coefs = lax.all_to_all(coefs, "cls", 0, 0, tiled=True)
    class_sums, wedge_sums = sums_call(col_ref, coefs, slot_pieces[0] + slot_pieces[1])
    return (
        posterior,
        class_sums.reshape(CLS_DEV, NSET, SLICE),
        wedge_sums.reshape(CLS_DEV, NSET, 64),
    )


def solution(mesh):
    return jax.shard_map(
        inner,
        mesh=mesh,
        in_specs=(
            P(("tomo", "cls"), None, None),
            P(("tomo", "cls")),
            P(("tomo", "cls")),
            P(("tomo", "cls"), None),
            P(("tomo", "cls"), None),
            P("tomo", None, None),
            P("cls", None, None),
        ),
        out_specs=(P(("tomo", "cls"), None), P("cls", None, "tomo"), P("cls", None, "tomo")),
        check_vma=False,
    )
```
